512 devices in a mesh: head: 8 (over x, core), seq: 64 (over z, y).
Axes of the slice: x: 4, y: 4, z: 16, core: 2. Of those that a mesh axis runs over, the one named last changes fastest.
Arguments:
- activations: bfloat16 [8192, 4096], P('seq'), may hold values from -6 to 6
- w_query: bfloat16 [3, 4096, 2048], P(None, 'seq', 'head'), may hold values from -32 to 32
- w_keyval: bfloat16 [3, 4096, 1024], P(None, 'seq'), may hold values from -32 to 32
- q_gain: float32 [3, 2048], P(None, 'head'), may hold values from 0.1 to 1.9
- k_gain: float32 [3, 512], replicated, may hold values from 0.1 to 1.9
- stream_ids: int32 [8192], P('seq'), may hold values from 0 to 2
- local_times: int32 [8192], P('seq'), may hold values from 0 to 31
- block_map: int32 [128], replicated, may hold values from 0 to 127, each once
Outputs:
- attended: bfloat16 [8192, 2048], P('seq', 'head')
The draws below stay inside these ranges and needn't reach their ends.
Inputs may be any that keep to these rules, and one draw needn't show every extreme that they name: `block_map`: a permutation of the block indices.
All inputs are finite; a program needn't handle non-finite values.
Results may differ from the reference program's by a relative error of at most 0.012.
The reference program's roundings to bfloat16 on the way (of `values`, `q_normed` and `k_normed`) count: a program that leaves them out, or rounds other values in their place, can miss the bound.
Values may be sent and summed in bfloat16 or wider, within the bound.
A program may use at most 64 MiB of HBM per device.

```python
import math
import jax
import jax.numpy as jnp
from jax import lax

D = 4096
HEADS = 16
KV_HEADS = 4
HEAD_DIM = 128
STREAMS = 3
FRAMES = 32
ROWS_DEV = 128
TOKENS = 8192
BLOCK_ROWS = 64
BLOCKS = 128


def draw_activations(key, part):
    values = jax.random.normal(jax.random.fold_in(key, 301), (TOKENS, D), jnp.float32)
    return jnp.clip(values, -6.0, 6.0).astype(jnp.bfloat16)


def draw_w_query(key, part):
    base_draw = jnp.clip(jax.random.normal(jax.random.fold_in(key, 101), (STREAMS, D, HEADS * HEAD_DIM), jnp.float32), -6.0, 6.0) / jnp.sqrt(jnp.float32(D))
    return base_draw.astype(jnp.bfloat16)


def draw_w_keyval(key, part):
    base_draw = jnp.clip(jax.random.normal(jax.random.fold_in(key, 201), (STREAMS, D, 2 * KV_HEADS * HEAD_DIM), jnp.float32), -6.0, 6.0) / jnp.sqrt(jnp.float32(D))
    return base_draw.astype(jnp.bfloat16)


def draw_q_gain(key, part):
    values = 1.0 + 0.18 * jnp.clip(jax.random.normal(jax.random.fold_in(key, 401), (STREAMS, HEADS * HEAD_DIM), jnp.float32), -5.0, 5.0)
    return values


def draw_k_gain(key, part):
    values = 1.0 + 0.18 * jnp.clip(jax.random.normal(jax.random.fold_in(key, 501), (STREAMS, KV_HEADS * HEAD_DIM), jnp.float32), -5.0, 5.0)
    return values


def set_ends(values, key, smallest, largest):
    spot = [jax.random.randint(jax.random.fold_in(key, axis), (), 0, length) for axis, length in enumerate(values.shape)]
    main_axis = values.shape.index(max(values.shape))
    next_to = spot[:main_axis] + [(spot[main_axis] + 1) % values.shape[main_axis]] + spot[main_axis + 1:]
    return values.at[tuple(spot)].set(smallest).at[tuple(next_to)].set(largest)


def setup_inputs(seed: int = 0) -> dict:
    keys = jax.random.split(jax.random.key(seed), 9)
    activations = draw_activations(jax.random.fold_in(keys[8], 71), 0)
    w_query = draw_w_query(jax.random.fold_in(keys[8], 71), 0)
    w_keyval = draw_w_keyval(jax.random.fold_in(keys[8], 71), 0)
    q_gain = draw_q_gain(jax.random.fold_in(keys[8], 71), 0)
    k_gain = draw_k_gain(jax.random.fold_in(keys[8], 71), 0)
    stream_ids = set_ends(jax.random.randint(keys[5], (TOKENS,), 0, STREAMS), jax.random.fold_in(keys[5], 1), 0, STREAMS - 1).astype(jnp.int32)
    local_times = set_ends(jax.random.randint(keys[6], (TOKENS,), 0, FRAMES), jax.random.fold_in(keys[6], 1), 0, FRAMES - 1).astype(jnp.int32)
    block_map = jax.random.permutation(keys[7], BLOCKS).astype(jnp.int32)
    return dict(activations=activations, w_query=w_query, w_keyval=w_keyval, q_gain=q_gain, k_gain=k_gain, stream_ids=stream_ids, local_times=local_times, block_map=block_map)


epsilon = 1e-06

def reference(activations, w_query, w_keyval, q_gain, k_gain, stream_ids, local_times, block_map):
    group_size = HEADS // KV_HEADS
    stream_match = stream_ids[:, None] == jnp.arange(STREAMS, dtype=jnp.int32)[None, :]
    queries = jnp.zeros((TOKENS, HEADS * HEAD_DIM), jnp.float32)
    key_value = jnp.zeros((TOKENS, KV_HEADS * 2 * HEAD_DIM), jnp.float32)
    for stream in range(STREAMS):
        chosen = stream_match[:, stream:stream + 1]
        queries = queries + jnp.where(chosen, jnp.dot(activations, w_query[stream], preferred_element_type=jnp.float32), jnp.float32(0.0))
        key_value = key_value + jnp.where(chosen, jnp.dot(activations, w_keyval[stream], preferred_element_type=jnp.float32), jnp.float32(0.0))
    key_value = key_value.reshape(TOKENS, KV_HEADS, 2, HEAD_DIM)
    keys_raw = key_value[:, :, 0].reshape(TOKENS, KV_HEADS * HEAD_DIM)
    values = key_value[:, :, 1].astype(jnp.bfloat16)
    onehot = stream_match.astype(jnp.float32)
    q_scale = jnp.dot(onehot, q_gain, precision=lax.Precision.HIGHEST)
    k_scale = jnp.dot(onehot, k_gain, precision=lax.Precision.HIGHEST)
    q_normed = (queries * lax.rsqrt(lax.optimization_barrier(jnp.mean(queries * queries, axis=1)) + epsilon)[:, None] * q_scale).astype(jnp.bfloat16)
    q_normed = q_normed.reshape(TOKENS, KV_HEADS, group_size, HEAD_DIM)
    k_normed = (keys_raw * lax.rsqrt(lax.optimization_barrier(jnp.mean(keys_raw * keys_raw, axis=1)) + epsilon)[:, None] * k_scale).astype(jnp.bfloat16)
    k_normed = k_normed.reshape(TOKENS, KV_HEADS, HEAD_DIM)
    time_pos = block_map[jnp.arange(TOKENS, dtype=jnp.int32) // BLOCK_ROWS] * FRAMES + local_times
    key_float = k_normed.astype(jnp.float32)
    value_float = values.astype(jnp.float32)
    score_scale = 1.0 / math.sqrt(HEAD_DIM)
    block_count = TOKENS // ROWS_DEV

    def attend(inputs):
        query_block, query_times = inputs
        scores = jnp.einsum('rkgd,nkd->rkgn', query_block.astype(jnp.float32), key_float) * score_scale
        visible = time_pos[None, None, None, :] <= query_times[:, None, None, None]
        row_peak = lax.optimization_barrier(jnp.max(jnp.where(visible, scores, -1e+30), axis=3, keepdims=True))
        exp_terms = jnp.where(visible, jnp.exp(scores - row_peak), jnp.float32(0.0))
        row_total = lax.optimization_barrier(jnp.sum(exp_terms, axis=3))
        mixed_out = jnp.einsum('rkgn,nkd->rkgd', exp_terms.astype(jnp.bfloat16).astype(jnp.float32), value_float)
        return (mixed_out / row_total[..., None]).reshape(ROWS_DEV, HEADS * HEAD_DIM).astype(jnp.bfloat16)
    result = lax.map(attend, (q_normed.reshape(block_count, ROWS_DEV, KV_HEADS, group_size, HEAD_DIM), time_pos.reshape(block_count, ROWS_DEV)))
    return result.reshape(TOKENS, HEADS * HEAD_DIM)
```

```python
import math

import jax
import jax.numpy as jnp
from jax import lax
from jax.experimental import pallas as pl
from jax.experimental.pallas import tpu as pltpu
from jax.sharding import PartitionSpec as P

HEADS = 16
KV_HEADS = 4
HEAD_DIM = 128
STREAMS = 3
FRAMES = 32
EPS = 1e-06
MESH = pl.DeviceIdType.MESH

Z, Y, X = 16, 4, 4
ROWS = 128
SHARD = 64
HALF = ROWS // 2
DEPTH = Z * SHARD
COLS = 3 * HEAD_DIM
META = 128
KEYS = Z * ROWS
KROWS = ROWS + 16
NEG = -1e30

ORDER = [0]
for _k in range(1, Z // 2):
    ORDER += [_k, -_k]
ORDER.append(Z // 2)
POS = {o: i for i, o in enumerate(ORDER)}
POS[-Z // 2] = POS[Z // 2]


def to_row(col):
    return jnp.transpose(jnp.broadcast_to(col, (ROWS, 128)))[0:8, :]


def to_cols(row):
    return jnp.transpose(jnp.broadcast_to(row, (128, ROWS)))


def kernel(
    x_hbm, wq_hbm, wkv_hbm, qgain, kgain, meta, keymeta, out,
    xv, xpk, xall, wall, hot, acc_kv, acc_q, in_kv, in_q, statk, statq,
    kv2, qall, ktime, obuf, oin, lbuf, lin,
    load_sem, w_ss, w_rs, x_ss, x_rs, xp_ss, xp_rs, kv_ss, kv_rs, q_ss, q_rs,
    sk_ss, sk_rs, sq_ss, sq_rs, g_ss, g_rs, p_ss, p_rs, qa_ss, qa_rs,
    o_ss, o_rs, l_ss, l_rs,
):
    h = lax.axis_index("head")
    s = lax.axis_index("seq")
    x, c = h // 2, h % 2
    z, y = s // Y, s % Y

    def zdev(d):
        return (h, lax.rem(z + d + Z, Z) * Y + y)

    def ydev(d):
        return (h, z * Y + lax.rem(y + d + Y, Y))

    def hdev(d):
        return (lax.rem(h + d, 2 * X), s)

    def xdev(d):
        return (lax.rem(h + 2 * d, 2 * X), s)

    partner = (2 * x + 1 - c, s)

    def remote(src, dst, ss, rs, dev):
        return pltpu.make_async_remote_copy(
            src_ref=src, dst_ref=dst, send_sem=ss, recv_sem=rs,
            device_id=dev, device_id_type=MESH,
        )

    x_load = pltpu.make_async_copy(x_hbm, xv, load_sem.at[0])
    wq_load = pltpu.make_async_copy(
        wq_hbm, wall.at[:, pl.ds(0, SHARD), pl.ds(HEAD_DIM, 2 * HEAD_DIM)], load_sem.at[1])
    kv_off = pl.multiple_of((2 * x + c) * HEAD_DIM, HEAD_DIM)
    wkv_load = pltpu.make_async_copy(
        wkv_hbm.at[:, :, pl.ds(kv_off, HEAD_DIM)],
        wall.at[:, pl.ds(0, SHARD), pl.ds(0, HEAD_DIM)], load_sem.at[2])
    wkv_load.start()
    wq_load.start()
    x_load.start()
    barrier = pltpu.get_barrier_semaphore()
    peers = [zdev(d) for d in (1, -1, 2, -2, 3, -3)]
    peers += [ydev(d) for d in (1, 2, 3)]
    peers += [hdev(d) for d in range(1, 2 * X)]
    for dev in peers:
        pl.semaphore_signal(barrier, inc=1, device_id=dev, device_id_type=MESH)
    wkv_load.wait()
    wq_load.wait()
    pl.semaphore_wait(barrier, len(peers))

    def w_copy(k, j, up):
        sign = -1 if up else 1
        src = wall.at[j, pl.ds(POS[sign * (k - 1)] * SHARD, SHARD)]
        dst = wall.at[j, pl.ds(POS[sign * k] * SHARD, SHARD)]
        i = 0 if up else 1
        return remote(src, dst, w_ss.at[i, k - 1, j], w_rs.at[i, k - 1, j], zdev(1 if up else -1))

    last = Z // 2
    ways = {}
    for k in range(1, last):
        ways[k] = [(j, up) for j in range(STREAMS) for up in (True, False)]
    ways[last] = [(0, True), (2, False), (1, True)]
    w_live = {}

    def w_step(k):
        for j, up in ways[k]:
            if k > 1:
                w_live[(k - 1, j, up)].wait_recv()
            w_live[(k, j, up)] = w_copy(k, j, up)
            w_live[(k, j, up)].start()
        if k == last:
            for j, up in ways[k - 1]:
                if (j, up) not in ways[k]:
                    w_live[(k - 1, j, up)].wait_recv()

    sends = []

    def sent(copy):
        copy.start()
        sends.append(copy)
        return copy

    w_step(1)

    x_load.wait()
    for t in range(Y):
        half = t % 2
        for pair in range(Z // 2):
            parts = []
            for o in (ORDER[2 * pair], ORDER[2 * pair + 1]):
                tile = 2 * lax.rem(z + o + Z, Z) + t // 2
                block = xv[:, pl.ds(pl.multiple_of(tile * 128, 128), 128)]
                parts.append(block[:, half * SHARD:(half + 1) * SHARD])
            xpk[t, :, pl.ds(pair * 128, 128)] = jnp.concatenate(parts, axis=1)
        xpk[t, :, pl.ds(DEPTH, META)] = meta[...]
    w_step(2)
    my_half = pl.ds(pl.multiple_of(c * HALF, HALF), HALF)
    x_live = {}
    for d in (2, 1, 3):
        x_live[d] = sent(remote(
            xpk.at[lax.rem(y + d, Y), my_half], xall.at[d, my_half],
            x_ss.at[d - 1], x_rs.at[d - 1], ydev(d)))
    xall[0] = xpk[y]
    w_step(3)
    w_step(4)
    xp_live = []
    for d in (1, 3, 2):
        x_live[d].wait_recv()
        xp_live.append(sent(remote(
            xall.at[d, my_half], xall.at[d, my_half],
            xp_ss.at[d - 1], xp_rs.at[d - 1], partner)))
    w_step(5)
    for copy in xp_live:
        copy.wait_recv()
    for d in range(Y):
        sid = xall[d, :, pl.ds(DEPTH, META)][:, 0:1].astype(jnp.float32)
        for j in range(STREAMS):
            on = jnp.where(sid == jnp.float32(j), jnp.float32(1.0), jnp.float32(0.0))
            hot[j, pl.ds(d * ROWS, ROWS)] = jnp.broadcast_to(on, (ROWS, 256)).astype(jnp.bfloat16)

    def project(g):
        span = pl.ds(g * 256, 256)
        for d in range(Y):
            xs = xall[d, :, span]
            total = None
            for j in range(STREAMS):
                part = jnp.dot(
                    xs * hot[j, pl.ds(d * ROWS, ROWS)], wall[j, span, :],
                    preferred_element_type=jnp.float32)
                total = part if total is None else total + part
            if g == 0:
                acc_kv[d] = total[:, :HEAD_DIM]
                acc_q[d] = total[:, HEAD_DIM:]
            else:
                acc_kv[d] += total[:, :HEAD_DIM]
                acc_q[d] += total[:, HEAD_DIM:]

    project(0)
    w_step(6)
    project(1)
    w_step(7)
    project(2)
    w_step(8)
    for j, up in ways[last]:
        w_live[(last, j, up)].wait_recv()
    project(3)

    kv_live, q_live = [], []
    for d in (2, 1, 3):
        kv_live.append(sent(remote(
            acc_kv.at[d], in_kv.at[d - 1], kv_ss.at[d - 1], kv_rs.at[d - 1], ydev(-d))))
    for d in (2, 1, 3):
        q_live.append(sent(remote(
            acc_q.at[d], in_q.at[d - 1], q_ss.at[d - 1], q_rs.at[d - 1], ydev(-d))))
    for copy in kv_live:
        copy.wait_recv()
    kv = (acc_kv[0] + in_kv[0]) + (in_kv[1] + in_kv[2])
    statk[0] = to_row(jnp.sum(kv * kv, axis=1, keepdims=True))
    sk_live = []
    for d in (2, 1, 3):
        sk_live.append(sent(remote(
            statk.at[0], statk.at[d], sk_ss.at[d - 1], sk_rs.at[d - 1], xdev(d))))
    sid = meta[:, 0:1].astype(jnp.float32)
    k_scale = jnp.zeros((ROWS, HEAD_DIM), jnp.float32)
    q_scale = jnp.zeros((ROWS, 2 * HEAD_DIM), jnp.float32)
    group = pl.ds(pl.multiple_of(x * HEAD_DIM, HEAD_DIM), HEAD_DIM)
    for j in range(STREAMS):
        k_scale = jnp.where(sid == jnp.float32(j), kgain[j:j + 1, group], k_scale)
        q_scale = jnp.where(sid == jnp.float32(j), qgain[j:j + 1, :], q_scale)
    for copy in sk_live:
        copy.wait_recv()
    k_sq = (statk[0] + statk[1]) + (statk[2] + statk[3])
    k_rs = to_cols(lax.rsqrt(k_sq / (KV_HEADS * HEAD_DIM) + EPS)[0:1, :])
    is_key = c == 0
    normed = jnp.where(is_key, kv * k_rs * k_scale, kv)
    kv2[c, 0, pl.ds(0, ROWS)] = normed.astype(jnp.bfloat16)
    kv2[c, 0, pl.ds(ROWS, 16)] = keymeta[...]

    g_live, p_live = {}, {}
    full = pl.ds(0, KROWS)

    def g_send(have, step, rows=full, index=None):
        o = have - step
        o = o - Z if o > Z // 2 else o
        i = POS[o] if index is None else index
        g_live[i] = sent(remote(
            kv2.at[c, POS[have], rows], kv2.at[c, POS[o], rows],
            g_ss.at[i], g_rs.at[i], zdev(step)))

    def p_send(have):
        i = POS[have]
        p_live[i] = sent(remote(kv2.at[c, i], kv2.at[c, i], p_ss.at[i], p_rs.at[i], partner))

    def g_wait(o):
        g_live[POS[o]].wait_recv()

    for step in (3, -3, 1, -1):
        g_send(0, step)
    p_send(0)

    for copy in q_live:
        copy.wait_recv()
    q = (acc_q[0] + in_q[0]) + (in_q[1] + in_q[2])
    statq[0] = to_row(jnp.sum(q * q, axis=1, keepdims=True))
    sq_live = []
    for d in range(1, 2 * X):
        sq_live.append(sent(remote(
            statq.at[0], statq.at[d], sq_ss.at[d - 1], sq_rs.at[d - 1], hdev(d))))
    g_wait(3)
    g_send(3, -3)
    g_send(3, 1)
    g_send(3, -1)
    g_wait(-3)
    g_send(-3, 3)
    g_send(-3, -1)
    g_send(-3, 1)
    p_send(3)
    p_send(-3)
    for o in (1, -1):
        g_wait(o)
        p_send(o)
    for copy in sq_live:
        copy.wait_recv()
    q_sq = statq[0]
    for d in range(1, 2 * X):
        q_sq = q_sq + statq[d]
    q_rs = to_cols(lax.rsqrt(q_sq / (HEADS * HEAD_DIM) + EPS)[0:1, :])
    q_rs = jnp.concatenate([q_rs, q_rs], axis=1)
    qall[0] = (q * q_rs * q_scale).astype(jnp.bfloat16)
    qa_live = []
    for d in (2, 1, 3):
        qa_live.append(sent(remote(
            qall.at[0], qall.at[d], qa_ss.at[d - 1], qa_rs.at[d - 1], ydev(d))))
    low, high = pl.ds(0, HALF), pl.ds(HALF, KROWS - HALF)
    g_wait(6)
    g_send(6, -2, low, Z - 1)
    g_send(6, 1)
    g_send(6, -1)
    g_wait(-6)
    g_send(-6, 2, high, Z)
    g_send(-6, -1)
    g_send(-6, 1)
    p_send(6)
    p_send(-6)
    for o in (2, 4, -2, -4, 5, 7, -5, -7):
        g_wait(o)
        p_send(o)
    g_live[Z - 1].wait_recv()
    g_live[Z].wait_recv()
    p_send(Z // 2)
    for copy in qa_live:
        copy.wait_recv()
    for copy in p_live.values():
        copy.wait_recv()

    for i in range(Z):
        km = kv2[0, i, pl.ds(ROWS, 16)].astype(jnp.float32)
        ktime[0:1, pl.ds(i * ROWS, ROWS)] = km[1:2, :] * FRAMES + km[0:1, :]

    score_scale = 1.0 / math.sqrt(HEAD_DIM)

    def o_copy(d):
        return remote(obuf.at[d], oin.at[d], o_ss.at[d], o_rs.at[d], ydev(-d))

    def l_copy(d):
        return remote(lbuf.at[d], lin.at[d], l_ss.at[d], l_rs.at[d], ydev(-d))

    def attend(i, carry):
        d = Y - 1 - i
        qm = xall[d, :, pl.ds(DEPTH, META)].astype(jnp.float32)
        qtime = qm[:, 64:65] * FRAMES + qm[:, 32:33]
        keys = kv2[0, :, pl.ds(0, ROWS), :].reshape(KEYS, HEAD_DIM)
        values = kv2[1, :, pl.ds(0, ROWS), :].reshape(KEYS, HEAD_DIM)
        for n in range(2):
            qn = qall[d, :, pl.ds(n * HEAD_DIM, HEAD_DIM)]
            scores = lax.dot_general(
                qn, keys, (((1,), (1,)), ((), ())), preferred_element_type=jnp.float32)
            scores = jnp.where(ktime[0:1, :] <= qtime, scores * score_scale, NEG)
            peak = jnp.max(scores, axis=1, keepdims=True)
            terms = jnp.exp(scores - peak)
            total = jnp.sum(terms, axis=1, keepdims=True)
            mixed = jnp.dot(
                terms.astype(jnp.bfloat16), values, preferred_element_type=jnp.float32)
            obuf[d, :, pl.ds(n * HEAD_DIM, HEAD_DIM)] = (mixed / total).astype(jnp.bfloat16)
            lse = jnp.where(peak > 0.5 * NEG, peak + jnp.log(total), NEG)
            lbuf[d, pl.ds(n * 8, 8)] = to_row(lse)

        @pl.when(d > 0)
        def _():
            o_copy(d).start()
            l_copy(d).start()

        return carry

    lax.fori_loop(0, Y, attend, 0)
    oin[0] = obuf[0]
    lin[0] = lbuf[0]
    for d in range(1, Y):
        o_copy(d).wait_recv()
        l_copy(d).wait_recv()
    top = jnp.maximum(jnp.maximum(lin[0], lin[1]), jnp.maximum(lin[2], lin[3]))
    weights = [jnp.exp(lin[d] - top) for d in range(Y)]
    norm = 1.0 / ((weights[0] + weights[1]) + (weights[2] + weights[3]))
    for n in range(2):
        span = pl.ds(n * HEAD_DIM, HEAD_DIM)
        result = None
        for d in range(Y):
            w = to_cols((weights[d] * norm)[n * 8:n * 8 + 1, :])
            part = w * oin[d, :, span].astype(jnp.float32)
            result = part if result is None else result + part
        out[:, span] = result.astype(jnp.bfloat16)

    for copy in w_live.values():
        copy.wait_send()
    for copy in sends:
        copy.wait_send()
    for d in range(1, Y):
        o_copy(d).wait_send()
        l_copy(d).wait_send()


def body(activations, w_query, w_keyval, q_gain, k_gain, stream_ids, local_times, block_map):
    position = lax.axis_index("seq")
    lane = lax.broadcasted_iota(jnp.int32, (ROWS, META), 1)
    row_block = 2 * position + jnp.arange(ROWS, dtype=jnp.int32) // (ROWS // 2)
    match = row_block[:, None] == jnp.arange(block_map.shape[0], dtype=jnp.int32)[None, :]
    place = jnp.sum(jnp.where(match, block_map[None, :], 0), axis=1)
    meta = jnp.where(
        lane < 32, stream_ids[:, None], jnp.where(lane < 64, local_times[:, None], place[:, None])
    ).astype(jnp.bfloat16)
    line = lax.broadcasted_iota(jnp.int32, (16, ROWS), 0)
    keymeta = jnp.where(line == 0, local_times[None, :], place[None, :]).astype(jnp.bfloat16)

    bf, f32 = jnp.bfloat16, jnp.float32
    vmem = pl.BlockSpec(memory_space=pltpu.VMEM)
    anywhere = pl.BlockSpec(memory_space=pl.ANY)
    dma = pltpu.SemaphoreType.DMA
    scratch = [
        pltpu.VMEM((ROWS, 4096), bf),
        pltpu.VMEM((Y, ROWS, DEPTH + META), bf),
        pltpu.VMEM((Y, ROWS, DEPTH + META), bf),
        pltpu.VMEM((STREAMS, DEPTH, COLS), bf),
        pltpu.VMEM((STREAMS, Y * ROWS, 256), bf),
        pltpu.VMEM((Y, ROWS, HEAD_DIM), f32),
        pltpu.VMEM((Y, ROWS, 2 * HEAD_DIM), f32),
        pltpu.VMEM((Y - 1, ROWS, HEAD_DIM), f32),
        pltpu.VMEM((Y - 1, ROWS, 2 * HEAD_DIM), f32),
        pltpu.VMEM((X, 8, ROWS), f32),
        pltpu.VMEM((2 * X, 8, ROWS), f32),
        pltpu.VMEM((2, Z, KROWS, HEAD_DIM), bf),
        pltpu.VMEM((Y, ROWS, 2 * HEAD_DIM), bf),
        pltpu.VMEM((8, KEYS), f32),
        pltpu.VMEM((Y, ROWS, 2 * HEAD_DIM), bf),
        pltpu.VMEM((Y, ROWS, 2 * HEAD_DIM), bf),
        pltpu.VMEM((Y, 16, ROWS), f32),
        pltpu.VMEM((Y, 16, ROWS), f32),
        dma((3,)),
        dma((2, Z // 2, STREAMS)), dma((2, Z // 2, STREAMS)),
    ]
    for n in (3, 3, 3, 3, 3, 7, Z + 1, Z, 3, 4, 4):
        scratch += [dma((n,)), dma((n,))]
    return pl.pallas_call(
        kernel,
        out_shape=jax.ShapeDtypeStruct((ROWS, 2 * HEAD_DIM), bf),
        in_specs=[anywhere, anywhere, anywhere, vmem, vmem, vmem, vmem],
        out_specs=vmem,
        scratch_shapes=scratch,
        compiler_params=pltpu.CompilerParams(
            collective_id=0, has_side_effects=True, vmem_limit_bytes=56 << 20),
        name="duplex_attention",
    )(activations, w_query, w_keyval, q_gain, k_gain, meta, keymeta)


def solution(mesh):
    placed = (
        P("seq", None),
        P(None, "seq", "head"),
        P(None, "seq", None),
        P(None, "head"),
        P(),
        P("seq"),
        P("seq"),
        P(),
    )
    return jax.shard_map(
        body, mesh=mesh, in_specs=placed, out_specs=P("seq", "head"), check_vma=False
    )
```

```python
import math

import jax
import jax.numpy as jnp
from jax import lax
from jax.experimental import pallas as pl
from jax.experimental.pallas import tpu as pltpu
from jax.sharding import PartitionSpec as P

HEADS = 16
KV_HEADS = 4
HEAD_DIM = 128
STREAMS = 3
FRAMES = 32
EPS = 1e-06
MESH = pl.DeviceIdType.MESH

Z, Y, X = 16, 4, 4
ROWS = 128
SHARD = 64
HALF = ROWS // 2
DEPTH = Z * SHARD
META = 128
KEYS = Z * ROWS
KROWS = ROWS + 16
NEG = -1e30

ORDER = [0]
for _k in range(1, Z // 2):
    ORDER += [_k, -_k]
ORDER.append(Z // 2)
POS = {o: i for i, o in enumerate(ORDER)}
POS[-Z // 2] = POS[Z // 2]


def to_row(col):
    return jnp.transpose(jnp.broadcast_to(col, (ROWS, 128)))[0:8, :]


def to_cols(row):
    return jnp.transpose(jnp.broadcast_to(row, (128, ROWS)))


def kernel(
    x_hbm, wq_hbm, wkv_hbm, qg_hbm, kg_hbm, ids_hbm, times_hbm, map_hbm, out,
    xv, qgain, kgain, ids, times, places, meta, xpk, xall, wall, wkv, hot, acc_kv, acc_q, in_kv, in_q, statk, statq,
    kv2, qall, ktime, obuf, oin, lbuf, lin,
    load_sem, w_ss, w_rs, x_ss, x_rs, xp_ss, xp_rs, kv_ss, kv_rs, q_ss, q_rs,
    sk_ss, sk_rs, sq_ss, sq_rs, g_ss, g_rs, p_ss, p_rs, qa_ss, qa_rs,
    o_ss, o_rs, l_ss, l_rs,
):
    h = lax.axis_index("head")
    s = lax.axis_index("seq")
    x, c = h // 2, h % 2
    z, y = s // Y, s % Y

    def zdev(d):
        return (h, lax.rem(z + d + Z, Z) * Y + y)

    def ydev(d):
        return (h, z * Y + lax.rem(y + d + Y, Y))

    def hdev(d):
        return (lax.rem(h + d, 2 * X), s)

    def xdev(d):
        return (lax.rem(h + 2 * d, 2 * X), s)

    partner = (2 * x + 1 - c, s)

    def remote(src, dst, ss, rs, dev):
        return pltpu.make_async_remote_copy(
            src_ref=src, dst_ref=dst, send_sem=ss, recv_sem=rs,
            device_id=dev, device_id_type=MESH,
        )

    kv_off = pl.multiple_of((2 * x + c) * HEAD_DIM, HEAD_DIM)
    w_loads = [
        (wkv_hbm.at[j, :, pl.ds(kv_off, HEAD_DIM)],
         wkv.at[pl.ds(0, SHARD), pl.ds(j * HEAD_DIM, HEAD_DIM)])
        for j in range(STREAMS)
    ]
    w_loads.append((wq_hbm, wall.at[:, pl.ds(0, SHARD)]))
    row_loads = [
        (x_hbm, xv), (ids_hbm, ids), (times_hbm, times), (map_hbm, places),
        (qg_hbm, qgain), (kg_hbm, kgain),
    ]
    loads = [
        pltpu.make_async_copy(src, dst, load_sem.at[i])
        for i, (src, dst) in enumerate(w_loads + row_loads)
    ]
    for load in loads:
        load.start()
    barrier = pltpu.get_barrier_semaphore()
    peers = [zdev(d) for d in (1, -1, 2, -2, 3, -3, 6, -6)]
    peers += [ydev(d) for d in (1, 2, 3)]
    peers += [hdev(d) for d in range(1, 2 * X)]
    for dev in peers:
        pl.semaphore_signal(barrier, inc=1, device_id=dev, device_id_type=MESH)
    for load in loads[:len(w_loads)]:
        load.wait()
    pl.semaphore_wait(barrier, len(peers))

    sends = []

    def sent(copy):
        copy.start()
        sends.append(copy)
        return copy

    class Spread:
        def __init__(self, piece, ss, rs):
            self.piece, self.ss, self.rs, self.live = piece, ss, rs, {}

        def send(self, have, step, part=0, index=None):
            o = have - step
            o = o - Z if o > Z // 2 else o
            i = POS[o] if index is None else index
            self.live[i] = sent(remote(
                self.piece(POS[have], part), self.piece(POS[o], part),
                self.ss.at[i], self.rs.at[i], zdev(step)))

        def wait(self, o):
            self.live[POS[o]].wait_recv()

        def first(self):
            for step in (6, -6, 3, -3, 1, -1):
                self.send(0, step)

        def second(self):
            for o in (3, -3):
                self.wait(o)
                self.send(o, 1)
                self.send(o, -1)

        def third(self):
            for o in (6, -6):
                self.wait(o)
                self.send(o, 1)
                self.send(o, -1)
            self.send(6, -2, 1, Z - 1)
            self.send(-6, 2, 2, Z)

        def wait_last(self):
            self.live[Z - 1].wait_recv()
            self.live[Z].wait_recv()

    def kv_piece(i, part):
        start, size = ((0, KROWS), (0, HALF), (HALF, KROWS - HALF))[part]
        return kv2.at[c, i, pl.ds(start, size)]

    kv_spread = Spread(kv_piece, g_ss, g_rs)

    def w_piece(i, j):
        span = pl.ds(i * SHARD, SHARD)
        return wkv.at[span] if j == 0 else wall.at[j - 1, span]

    def w_copy(k, j, up):
        sign = -1 if up else 1
        src, dst = w_piece(POS[sign * (k - 1)], j), w_piece(POS[sign * k], j)
        i = 0 if up else 1
        return remote(src, dst, w_ss.at[i, k - 1, j], w_rs.at[i, k - 1, j], zdev(1 if up else -1))

    last = Z // 2
    ways = {}
    for k in range(1, last):
        ways[k] = [(j, up) for j in range(STREAMS + 1) for up in (True, False)]
    ways[last] = [(0, True), (1, False), (2, True), (3, False)]
    w_live = {}

    def w_step(k):
        for j, up in ways[k]:
            if k > 1:
                w_live[(k - 1, j, up)].wait_recv()
            w_live[(k, j, up)] = w_copy(k, j, up)
            w_live[(k, j, up)].start()

    def w_done(j):
        for k in (last - 1, last):
            for i, up in ways[k]:
                if i == j and (k == last or (j, up) not in ways[last]):
                    w_live[(k, j, up)].wait_recv()

    w_step(1)
    for load in loads[len(w_loads):]:
        load.wait()

    lane = lax.broadcasted_iota(jnp.int32, (ROWS, META), 1)
    row_lane = lax.broadcasted_iota(jnp.int32, (1, ROWS), 1)
    block_places = places[...].astype(jnp.float32)
    first, second = [
        jnp.sum(jnp.where(row_lane == 2 * s + i, block_places, 0.0), axis=1, keepdims=True)
        for i in range(2)
    ]
    place_row = jnp.where(row_lane < HALF, first, second)
    time_row = times[...].astype(jnp.float32)
    id_col = to_cols(ids[...].astype(jnp.float32))
    meta[...] = jnp.where(
        lane < 32, id_col, jnp.where(lane < 64, to_cols(time_row), to_cols(place_row))
    ).astype(jnp.bfloat16)

    for t in range(Y):
        half = t % 2
        for pair in range(Z // 2):
            parts = []
            for o in (ORDER[2 * pair], ORDER[2 * pair + 1]):
                tile = 2 * lax.rem(z + o + Z, Z) + t // 2
                block = xv[:, pl.ds(pl.multiple_of(tile * 128, 128), 128)]
                parts.append(block[:, half * SHARD:(half + 1) * SHARD])
            xpk[t, :, pl.ds(pair * 128, 128)] = jnp.concatenate(parts, axis=1)
        xpk[t, :, pl.ds(DEPTH, META)] = meta[...]
    my_half = pl.ds(pl.multiple_of(c * HALF, HALF), HALF)
    x_live = {}
    for d in (2, 1, 3):
        x_live[d] = sent(remote(
            xpk.at[lax.rem(y + d, Y), my_half], xall.at[d, my_half],
            x_ss.at[d - 1], x_rs.at[d - 1], ydev(d)))
    xall[0] = xpk[y]
    w_step(2)
    w_step(3)
    xp_live = []
    for d in (1, 3, 2):
        x_live[d].wait_recv()
        xp_live.append(sent(remote(
            xall.at[d, my_half], xall.at[d, my_half],
            xp_ss.at[d - 1], xp_rs.at[d - 1], partner)))
    w_step(4)
    for copy in xp_live:
        copy.wait_recv()
    for d in range(Y):
        sid = xall[d, :, pl.ds(DEPTH, META)][:, 0:1].astype(jnp.float32)
        for j in range(STREAMS):
            on = jnp.where(sid == jnp.float32(j), jnp.float32(1.0), jnp.float32(0.0))
            hot[j, pl.ds(d * ROWS, ROWS)] = jnp.broadcast_to(on, (ROWS, 256)).astype(jnp.bfloat16)
    w_step(5)

    def project(g):
        span = pl.ds(g * 256, 256)
        for d in range(Y):
            xs = xall[d, :, span]
            total = None
            for j in range(STREAMS):
                part = jnp.dot(
                    xs * hot[j, pl.ds(d * ROWS, ROWS)], wall[j, span, :],
                    preferred_element_type=jnp.float32)
                total = part if total is None else total + part
            if g == 0:
                acc_q[d] = total
            else:
                acc_q[d] += total

    def project_kv(d, span):
        sid = xall[d, :, pl.ds(DEPTH, META)][:, 0:1].astype(jnp.float32)
        every = jnp.dot(xall[d, :, span], wkv[span, :], preferred_element_type=jnp.float32)
        part = every[:, :HEAD_DIM]
        for j in range(1, STREAMS):
            part = jnp.where(
                sid == jnp.float32(j), every[:, j * HEAD_DIM:(j + 1) * HEAD_DIM], part)
        return part

    early, late = pl.ds(0, DEPTH - 256), pl.ds(DEPTH - 256, 256)
    project(0)
    w_step(6)
    project(1)
    w_step(7)
    for d in range(Y):
        acc_kv[d] = project_kv(d, early)
    project(2)
    w_step(8)
    k_scale = jnp.zeros((ROWS, HEAD_DIM), jnp.float32)
    q_scale = jnp.zeros((ROWS, 2 * HEAD_DIM), jnp.float32)
    sid = meta[:, 0:1].astype(jnp.float32)
    group = pl.ds(pl.multiple_of(x * HEAD_DIM, HEAD_DIM), HEAD_DIM)
    for j in range(STREAMS):
        k_scale = jnp.where(sid == jnp.float32(j), kgain[j:j + 1, group], k_scale)
        q_scale = jnp.where(sid == jnp.float32(j), qgain[j:j + 1, :], q_scale)

    w_done(0)
    kv_live, q_live = [], []
    for d in (2, 1, 3, 0):
        acc_kv[d] += project_kv(d, late)
        if d:
            kv_live.append(sent(remote(
                acc_kv.at[d], in_kv.at[d - 1], kv_ss.at[d - 1], kv_rs.at[d - 1], ydev(-d))))
    for j in range(STREAMS):
        w_done(j + 1)
    project(3)
    for d in (2, 1, 3):
        q_live.append(sent(remote(
            acc_q.at[d], in_q.at[d - 1], q_ss.at[d - 1], q_rs.at[d - 1], ydev(-d))))
    for copy in kv_live:
        copy.wait_recv()
    kv = (acc_kv[0] + in_kv[0]) + (in_kv[1] + in_kv[2])
    statk[0] = to_row(jnp.sum(kv * kv, axis=1, keepdims=True))
    sk_live = []
    for d in (2, 1, 3):
        sk_live.append(sent(remote(
            statk.at[0], statk.at[d], sk_ss.at[d - 1], sk_rs.at[d - 1], xdev(d))))
    for copy in sk_live:
        copy.wait_recv()
    k_sq = (statk[0] + statk[1]) + (statk[2] + statk[3])
    k_rs = to_cols(lax.rsqrt(k_sq / (KV_HEADS * HEAD_DIM) + EPS)[0:1, :])
    is_key = c == 0
    normed = jnp.where(is_key, kv * k_rs * k_scale, kv)
    kv2[c, 0, pl.ds(0, ROWS)] = normed.astype(jnp.bfloat16)
    line = lax.broadcasted_iota(jnp.int32, (16, ROWS), 0)
    kv2[c, 0, pl.ds(ROWS, 16)] = jnp.where(line == 0, time_row, place_row).astype(jnp.bfloat16)

    p_live = {}

    def p_send(have):
        i = POS[have]
        p_live[i] = sent(remote(kv2.at[c, i], kv2.at[c, i], p_ss.at[i], p_rs.at[i], partner))

    kv_spread.first()
    p_send(0)
    for copy in q_live:
        copy.wait_recv()
    q = (acc_q[0] + in_q[0]) + (in_q[1] + in_q[2])
    statq[0] = to_row(jnp.sum(q * q, axis=1, keepdims=True))
    sq_live = []
    for d in range(1, 2 * X):
        sq_live.append(sent(remote(
            statq.at[0], statq.at[d], sq_ss.at[d - 1], sq_rs.at[d - 1], hdev(d))))
    kv_spread.second()
    p_send(3)
    p_send(-3)
    for o in (1, -1):
        kv_spread.wait(o)
        p_send(o)
    for copy in sq_live:
        copy.wait_recv()
    q_sq = statq[0]
    for d in range(1, 2 * X):
        q_sq = q_sq + statq[d]
    q_rs = to_cols(lax.rsqrt(q_sq / (HEADS * HEAD_DIM) + EPS)[0:1, :])
    q_rs = jnp.concatenate([q_rs, q_rs], axis=1)
    qall[0] = (q * q_rs * q_scale).astype(jnp.bfloat16)

    def qa_copy(d):
        return remote(qall.at[0], qall.at[d], qa_ss.at[d], qa_rs.at[d], ydev(d))

    for d in (2, 1, 3):
        qa_copy(d).start()
    kv_spread.third()
    p_send(6)
    p_send(-6)
    for o in (2, 4, -2, -4, 5, 7, -5, -7):
        kv_spread.wait(o)
        p_send(o)
    kv_spread.wait_last()
    p_send(Z // 2)
    for copy in p_live.values():
        copy.wait_recv()

    for i in range(Z):
        km = kv2[0, i, pl.ds(ROWS, 16)].astype(jnp.float32)
        ktime[0:1, pl.ds(i * ROWS, ROWS)] = km[1:2, :] * FRAMES + km[0:1, :]

    score_scale = 1.0 / math.sqrt(HEAD_DIM)

    def o_copy(d):
        return remote(obuf.at[d], oin.at[d], o_ss.at[d], o_rs.at[d], ydev(-d))

    def l_copy(d):
        return remote(lbuf.at[d], lin.at[d], l_ss.at[d], l_rs.at[d], ydev(-d))

    def attend(i, carry):
        d = Y - 1 - i

        @pl.when(d > 0)
        def _():
            qa_copy(d).wait_recv()

        qm = xall[d, :, pl.ds(DEPTH, META)].astype(jnp.float32)
        qtime = qm[:, 64:65] * FRAMES + qm[:, 32:33]
        keys = kv2[0, :, pl.ds(0, ROWS), :].reshape(KEYS, HEAD_DIM)
        values = kv2[1, :, pl.ds(0, ROWS), :].reshape(KEYS, HEAD_DIM)
        for n in range(2):
            qn = qall[d, :, pl.ds(n * HEAD_DIM, HEAD_DIM)]
            scores = lax.dot_general(
                qn, keys, (((1,), (1,)), ((), ())), preferred_element_type=jnp.float32)
            scores = jnp.where(ktime[0:1, :] <= qtime, scores * score_scale, NEG)
            peak = jnp.max(scores, axis=1, keepdims=True)
            terms = jnp.exp(scores - peak)
            total = jnp.sum(terms, axis=1, keepdims=True)
            mixed = jnp.dot(
                terms.astype(jnp.bfloat16), values, preferred_element_type=jnp.float32)
            obuf[d, :, pl.ds(n * HEAD_DIM, HEAD_DIM)] = (mixed / total).astype(jnp.bfloat16)
            lse = jnp.where(peak > 0.5 * NEG, peak + jnp.log(total), NEG)
            lbuf[d, pl.ds(n * 8, 8)] = to_row(lse)

        @pl.when(d > 0)
        def _():
            o_copy(d).start()
            l_copy(d).start()

        return carry

    lax.fori_loop(0, Y, attend, 0)
    oin[0] = obuf[0]
    lin[0] = lbuf[0]
    for d in range(1, Y):
        o_copy(d).wait_recv()
        l_copy(d).wait_recv()
    top = jnp.maximum(jnp.maximum(lin[0], lin[1]), jnp.maximum(lin[2], lin[3]))
    weights = [jnp.exp(lin[d] - top) for d in range(Y)]
    norm = 1.0 / ((weights[0] + weights[1]) + (weights[2] + weights[3]))
    for n in range(2):
        span = pl.ds(n * HEAD_DIM, HEAD_DIM)
        result = None
        for d in range(Y):
            w = to_cols((weights[d] * norm)[n * 8:n * 8 + 1, :])
            part = w * oin[d, :, span].astype(jnp.float32)
            result = part if result is None else result + part
        out[:, span] = result.astype(jnp.bfloat16)

    for copy in w_live.values():
        copy.wait_send()
    for copy in sends:
        copy.wait_send()
    for d in range(1, Y):
        qa_copy(d).wait_send()
        o_copy(d).wait_send()
        l_copy(d).wait_send()


def body(activations, w_query, w_keyval, q_gain, k_gain, stream_ids, local_times, block_map):
    bf, f32 = jnp.bfloat16, jnp.float32
    vmem = pl.BlockSpec(memory_space=pltpu.VMEM)
    anywhere = pl.BlockSpec(memory_space=pl.ANY)
    dma = pltpu.SemaphoreType.DMA
    scratch = [
        pltpu.VMEM((ROWS, 4096), bf),
        pltpu.VMEM((STREAMS, 2 * HEAD_DIM), f32),
        pltpu.VMEM((STREAMS, KV_HEADS * HEAD_DIM), f32),
        pltpu.VMEM((1, ROWS), jnp.int32),
        pltpu.VMEM((1, ROWS), jnp.int32),
        pltpu.VMEM((1, ROWS), jnp.int32),
        pltpu.VMEM((ROWS, META), bf),
        pltpu.VMEM((Y, ROWS, DEPTH + META), bf),
        pltpu.VMEM((Y, ROWS, DEPTH + META), bf),
        pltpu.VMEM((STREAMS, DEPTH, 2 * HEAD_DIM), bf),
        pltpu.VMEM((DEPTH, STREAMS * HEAD_DIM), bf),
        pltpu.VMEM((STREAMS, Y * ROWS, 256), bf),
        pltpu.VMEM((Y, ROWS, HEAD_DIM), f32),
        pltpu.VMEM((Y, ROWS, 2 * HEAD_DIM), f32),
        pltpu.VMEM((Y - 1, ROWS, HEAD_DIM), f32),
        pltpu.VMEM((Y - 1, ROWS, 2 * HEAD_DIM), f32),
        pltpu.VMEM((X, 8, ROWS), f32),
        pltpu.VMEM((2 * X, 8, ROWS), f32),
        pltpu.VMEM((2, Z, KROWS, HEAD_DIM), bf),
        pltpu.VMEM((Y, ROWS, 2 * HEAD_DIM), bf),
        pltpu.VMEM((8, KEYS), f32),
        pltpu.VMEM((Y, ROWS, 2 * HEAD_DIM), bf),
        pltpu.VMEM((Y, ROWS, 2 * HEAD_DIM), bf),
        pltpu.VMEM((Y, 16, ROWS), f32),
        pltpu.VMEM((Y, 16, ROWS), f32),
        dma((10,)),
        dma((2, Z // 2, STREAMS + 1)), dma((2, Z // 2, STREAMS + 1)),
    ]
    for n in (3, 3, 3, 3, 3, 7, Z + 1, Z, 4, 4, 4):
        scratch += [dma((n,)), dma((n,))]
    return pl.pallas_call(
        kernel,
        out_shape=pltpu.VMEM((ROWS, 2 * HEAD_DIM), bf),
        in_specs=[anywhere] * 8,
        out_specs=vmem,
        scratch_shapes=scratch,
        compiler_params=pltpu.CompilerParams(
            collective_id=0, has_side_effects=True, vmem_limit_bytes=56 << 20),
        name="duplex_attention",
    )(
        activations, w_query, w_keyval, q_gain, k_gain,
        stream_ids.reshape(1, ROWS), local_times.reshape(1, ROWS), block_map.reshape(1, ROWS),
    )


def solution(mesh):
    placed = (
        P("seq", None),
        P(None, "seq", "head"),
        P(None, "seq", None),
        P(None, "head"),
        P(),
        P("seq"),
        P("seq"),
        P(),
    )
    return jax.shard_map(
        body, mesh=mesh, in_specs=placed, out_specs=P("seq", "head"), check_vma=False
    )
```

```python
import math

import jax
import jax.numpy as jnp
from jax import lax
from jax.experimental import pallas as pl
from jax.experimental.pallas import tpu as pltpu
from jax.sharding import PartitionSpec as P

HEADS = 16
KV_HEADS = 4
HEAD_DIM = 128
STREAMS = 3
FRAMES = 32
EPS = 1e-06
MESH = pl.DeviceIdType.MESH

Z, Y, X = 16, 4, 4
ROWS = 128
SHARD = 64
HALF = ROWS // 2
DEPTH = Z * SHARD
META = 128
KEYS = Z * ROWS
NEG = -1e30
LOG2E = 1.0 / math.log(2.0)

ORDER = [0]
for _k in range(1, Z // 2):
    ORDER += [_k, -_k]
ORDER.append(Z // 2)
POS = {o: i for i, o in enumerate(ORDER)}
POS[-Z // 2] = POS[Z // 2]


def to_row(col):
    return jnp.transpose(jnp.broadcast_to(col, (ROWS, 128)))[0:8, :]


def to_cols(row):
    return jnp.transpose(jnp.broadcast_to(row, (128, ROWS)))


def kernel(
    x_hbm, wq_hbm, wkv_hbm, qg_hbm, kg_hbm, ids_hbm, times_hbm, map_hbm, out,
    xv, qgain, kgain, ids, times, places, meta, xpk, xall, wall, wkv, hot, acc_kv, acc_q, in_kv, in_q, statk, statq,
    kv2, when, qall, ktime, obuf, oin, lbuf, lin,
    load_sem, w_ss, w_rs, x_ss, x_rs, xp_ss, xp_rs, kv_ss, kv_rs, q_ss, q_rs,
    sk_ss, sk_rs, sq_ss, sq_rs, g_ss, g_rs, p_ss, p_rs, qa_ss, qa_rs,
    o_ss, o_rs, l_ss, l_rs,
):
    h = lax.axis_index("head")
    s = lax.axis_index("seq")
    x, c = h // 2, h % 2
    z, y = s // Y, s % Y

    def zdev(d):
        return (h, lax.rem(z + d + Z, Z) * Y + y)

    def ydev(d):
        return (h, z * Y + lax.rem(y + d + Y, Y))

    def hdev(d):
        return (lax.rem(h + d, 2 * X), s)

    def xdev(d):
        return (lax.rem(h + 2 * d, 2 * X), s)

    partner = (2 * x + 1 - c, s)

    def remote(src, dst, ss, rs, dev):
        return pltpu.make_async_remote_copy(
            src_ref=src, dst_ref=dst, send_sem=ss, recv_sem=rs,
            device_id=dev, device_id_type=MESH,
        )

    kv_off = pl.multiple_of((2 * x + c) * HEAD_DIM, HEAD_DIM)
    w_loads = [
        (wkv_hbm.at[j, :, pl.ds(kv_off, HEAD_DIM)],
         wkv.at[pl.ds(0, SHARD), pl.ds(j * HEAD_DIM, HEAD_DIM)])
        for j in range(STREAMS)
    ]
    w_loads.append((wq_hbm, wall.at[:, pl.ds(0, SHARD)]))
    row_loads = [
        (x_hbm, xv), (ids_hbm, ids), (times_hbm, times), (map_hbm, places),
        (qg_hbm, qgain), (kg_hbm, kgain),
    ]
    loads = [
        pltpu.make_async_copy(src, dst, load_sem.at[i])
        for i, (src, dst) in enumerate(w_loads + row_loads)
    ]
    for load in loads:
        load.start()
    barrier = pltpu.get_barrier_semaphore()
    peers = [zdev(d) for d in (1, -1)]
    peers += [ydev(d) for d in (1, 2, 3)]
    peers += [hdev(d) for d in range(1, 2 * X)]
    for dev in peers:
        pl.semaphore_signal(barrier, inc=1, device_id=dev, device_id_type=MESH)
    for load in loads[:len(w_loads)]:
        load.wait()
    pl.semaphore_wait(barrier, len(peers))

    sends = []

    def sent(copy):
        copy.start()
        sends.append(copy)
        return copy

    class Spread:
        def __init__(self, piece, ss, rs):
            self.piece, self.ss, self.rs, self.live = piece, ss, rs, {}

        def send(self, have, step, part=0, index=None):
            o = have - step
            o = o - Z if o > Z // 2 else o
            i = POS[o] if index is None else index
            self.live[i] = sent(remote(
                self.piece(POS[have], part), self.piece(POS[o], part),
                self.ss.at[i], self.rs.at[i], zdev(step)))

        def wait(self, o):
            self.live[POS[o]].wait_recv()

        def first(self):
            for step in (6, -6, 3, -3, 1, -1):
                self.send(0, step)

        def second(self):
            for o in (3, -3):
                self.wait(o)
                self.send(o, 1)
                self.send(o, -1)

        def third(self):
            for o in (6, -6):
                self.wait(o)
                self.send(o, 1)
                self.send(o, -1)
            self.send(6, -2, 1, Z - 1)
            self.send(-6, 2, 2, Z)

        def wait_last(self):
            self.live[Z - 1].wait_recv()
            self.live[Z].wait_recv()

    def kv_piece(i, part):
        start, size = ((0, ROWS), (0, HALF), (HALF, HALF))[part]
        return kv2.at[c, i, pl.ds(start, size)]

    kv_spread = Spread(kv_piece, g_ss, g_rs)

    def w_piece(i, j):
        span = pl.ds(i * SHARD, SHARD)
        if j == STREAMS + 1:
            return when.at[i]
        return wkv.at[span] if j == 0 else wall.at[j - 1, span]

    def w_copy(k, j, up):
        sign = -1 if up else 1
        src, dst = w_piece(POS[sign * (k - 1)], j), w_piece(POS[sign * k], j)
        i = 0 if up else 1
        return remote(src, dst, w_ss.at[i, k - 1, j], w_rs.at[i, k - 1, j], zdev(1 if up else -1))

    last = Z // 2
    ways = {}
    for k in range(1, last):
        ways[k] = [(j, up) for j in range(STREAMS + 2) for up in (True, False)]
    ways[last] = [(0, True), (1, False), (2, True), (3, False), (4, True)]
    w_live = {}

    def w_step(k, chunks=range(STREAMS + 2)):
        for j, up in ways[k]:
            if j not in chunks:
                continue
            if k > 1:
                w_live[(k - 1, j, up)].wait_recv()
            w_live[(k, j, up)] = w_copy(k, j, up)
            w_live[(k, j, up)].start()

    def w_done(j):
        for k in (last - 1, last):
            for i, up in ways[k]:
                if i == j and (k == last or (j, up) not in ways[last]):
                    w_live[(k, j, up)].wait_recv()

    w_step(1, range(STREAMS + 1))
    for load in loads[len(w_loads):]:
        load.wait()

    lane = lax.broadcasted_iota(jnp.int32, (ROWS, META), 1)
    row_lane = lax.broadcasted_iota(jnp.int32, (1, ROWS), 1)
    block_places = places[...].astype(jnp.float32)
    first, second = [
        jnp.sum(jnp.where(row_lane == 2 * s + i, block_places, 0.0), axis=1, keepdims=True)
        for i in range(2)
    ]
    place_row = jnp.where(row_lane < HALF, first, second)
    time_row = times[...].astype(jnp.float32)
    id_col = to_cols(ids[...].astype(jnp.float32))
    meta[...] = jnp.where(
        lane < 32, id_col, jnp.where(lane < 64, to_cols(time_row), to_cols(place_row))
    ).astype(jnp.bfloat16)

    line = lax.broadcasted_iota(jnp.int32, (16, ROWS), 0)
    when[0] = jnp.where(line == 0, time_row, place_row).astype(jnp.bfloat16)
    w_step(1, (STREAMS + 1,))

    for t in range(Y):
        half = t % 2
        for pair in range(Z // 2):
            parts = []
            for o in (ORDER[2 * pair], ORDER[2 * pair + 1]):
                tile = 2 * lax.rem(z + o + Z, Z) + t // 2
                block = xv[:, pl.ds(pl.multiple_of(tile * 128, 128), 128)]
                parts.append(block[:, half * SHARD:(half + 1) * SHARD])
            xpk[t, :, pl.ds(pair * 128, 128)] = jnp.concatenate(parts, axis=1)
        xpk[t, :, pl.ds(DEPTH, META)] = meta[...]
    my_half = pl.ds(pl.multiple_of(c * HALF, HALF), HALF)
    x_live = {}
    for d in (2, 1, 3):
        x_live[d] = sent(remote(
            xpk.at[lax.rem(y + d, Y), my_half], xall.at[d, my_half],
            x_ss.at[d - 1], x_rs.at[d - 1], ydev(d)))
    xall[0] = xpk[y]
    w_step(2)
    w_step(3)
    xp_live = []
    for d in (1, 3, 2):
        x_live[d].wait_recv()
        xp_live.append(sent(remote(
            xall.at[d, my_half], xall.at[d, my_half],
            xp_ss.at[d - 1], xp_rs.at[d - 1], partner)))
    w_step(4)
    for copy in xp_live:
        copy.wait_recv()
    for d in range(Y):
        sid = xall[d, :, pl.ds(DEPTH, META)][:, 0:1].astype(jnp.float32)
        for j in range(STREAMS):
            on = jnp.where(sid == jnp.float32(j), jnp.float32(1.0), jnp.float32(0.0))
            hot[j, pl.ds(d * ROWS, ROWS)] = jnp.broadcast_to(on, (ROWS, 256)).astype(jnp.bfloat16)
    w_step(5)

    def project(g):
        span = pl.ds(g * 256, 256)
        for d in range(Y):
            xs = xall[d, :, span]
            total = None
            for j in range(STREAMS):
                part = jnp.dot(
                    xs * hot[j, pl.ds(d * ROWS, ROWS)], wall[j, span, :],
                    preferred_element_type=jnp.float32)
                total = part if total is None else total + part
            if g == 0:
                acc_q[d] = total
            else:
                acc_q[d] += total

    def project_kv(d, span):
        sid = xall[d, :, pl.ds(DEPTH, META)][:, 0:1].astype(jnp.float32)
        every = jnp.dot(xall[d, :, span], wkv[span, :], preferred_element_type=jnp.float32)
        part = every[:, :HEAD_DIM]
        for j in range(1, STREAMS):
            part = jnp.where(
                sid == jnp.float32(j), every[:, j * HEAD_DIM:(j + 1) * HEAD_DIM], part)
        return part

    early, late = pl.ds(0, DEPTH - 256), pl.ds(DEPTH - 256, 256)
    project(0)
    w_step(6)
    project(1)
    w_step(7)
    for d in range(Y):
        acc_kv[d] = project_kv(d, early)
    project(2)
    w_step(8)
    k_scale = jnp.zeros((ROWS, HEAD_DIM), jnp.float32)
    q_scale = jnp.zeros((ROWS, 2 * HEAD_DIM), jnp.float32)
    sid = meta[:, 0:1].astype(jnp.float32)
    group = pl.ds(pl.multiple_of(x * HEAD_DIM, HEAD_DIM), HEAD_DIM)
    for j in range(STREAMS):
        k_scale = jnp.where(sid == jnp.float32(j), kgain[j:j + 1, group], k_scale)
        q_scale = jnp.where(sid == jnp.float32(j), qgain[j:j + 1, :], q_scale)

    w_done(0)
    kv_live, q_live = [], []
    for d in (2, 1, 3, 0):
        acc_kv[d] += project_kv(d, late)
        if d:
            kv_live.append(sent(remote(
                acc_kv.at[d], in_kv.at[d - 1], kv_ss.at[d - 1], kv_rs.at[d - 1], ydev(-d))))
    for j in range(STREAMS + 1):
        w_done(j + 1)
    project(3)
    for d in (2, 1, 3):
        q_live.append(sent(remote(
            acc_q.at[d], in_q.at[d - 1], q_ss.at[d - 1], q_rs.at[d - 1], ydev(-d))))
    for copy in kv_live:
        copy.wait_recv()
    kv = (acc_kv[0] + in_kv[0]) + (in_kv[1] + in_kv[2])
    statk[0] = to_row(jnp.sum(kv * kv, axis=1, keepdims=True))
    sk_live = []
    for d in (2, 1, 3):
        sk_live.append(sent(remote(
            statk.at[0], statk.at[d], sk_ss.at[d - 1], sk_rs.at[d - 1], xdev(d))))
    for copy in sk_live:
        copy.wait_recv()
    k_sq = (statk[0] + statk[1]) + (statk[2] + statk[3])
    k_rs = to_cols(lax.rsqrt(k_sq / (KV_HEADS * HEAD_DIM) + EPS)[0:1, :])
    is_key = c == 0
    normed = jnp.where(is_key, kv * k_rs * k_scale, kv)
    kv2[c, 0] = normed.astype(jnp.bfloat16)

    p_live = {}

    def p_send(have):
        i = POS[have]
        p_live[i] = sent(remote(kv2.at[c, i], kv2.at[c, i], p_ss.at[i], p_rs.at[i], partner))

    kv_spread.first()
    p_send(0)
    for copy in q_live:
        copy.wait_recv()
    q = (acc_q[0] + in_q[0]) + (in_q[1] + in_q[2])
    statq[0] = to_row(jnp.sum(q * q, axis=1, keepdims=True))
    sq_live = []
    for d in range(1, 2 * X):
        sq_live.append(sent(remote(
            statq.at[0], statq.at[d], sq_ss.at[d - 1], sq_rs.at[d - 1], hdev(d))))
    for i in range(Z):
        km = when[i].astype(jnp.float32)
        ktime[0:1, pl.ds(i * ROWS, ROWS)] = km[1:2, :] * FRAMES + km[0:1, :]
    kv_spread.second()
    p_send(3)
    p_send(-3)
    for o in (1, -1):
        kv_spread.wait(o)
        p_send(o)
    for copy in sq_live:
        copy.wait_recv()
    q_sq = statq[0]
    for d in range(1, 2 * X):
        q_sq = q_sq + statq[d]
    q_rs = to_cols(lax.rsqrt(q_sq / (HEADS * HEAD_DIM) + EPS)[0:1, :])
    q_rs = jnp.concatenate([q_rs, q_rs], axis=1)
    qall[0] = (q * q_rs * q_scale).astype(jnp.bfloat16)

    def qa_copy(d):
        return remote(qall.at[0], qall.at[d], qa_ss.at[d], qa_rs.at[d], ydev(d))

    for d in (2, 1, 3):
        qa_copy(d).start()
    kv_spread.third()
    p_send(6)
    p_send(-6)
    for o in (2, 4, -2, -4, 5, 7, -5, -7):
        kv_spread.wait(o)
        p_send(o)
    kv_spread.wait_last()
    p_send(Z // 2)
    for copy in p_live.values():
        copy.wait_recv()

    score_scale = 1.0 / math.sqrt(HEAD_DIM)

    def o_copy(d):
        return remote(obuf.at[d], oin.at[d], o_ss.at[d], o_rs.at[d], ydev(-d))

    def l_copy(d):
        return remote(lbuf.at[d], lin.at[d], l_ss.at[d], l_rs.at[d], ydev(-d))

    def attend(i, carry):
        d = Y - 1 - i

        @pl.when(d > 0)
        def _():
            qa_copy(d).wait_recv()

        qm = xall[d, :, pl.ds(DEPTH, META)].astype(jnp.float32)
        qtime = qm[:, 64:65] * FRAMES + qm[:, 32:33]
        keys = kv2[0].reshape(KEYS, HEAD_DIM)
        values = kv2[1].reshape(KEYS, HEAD_DIM)
        both = jnp.concatenate(
            [qall[d, :, pl.ds(n * HEAD_DIM, HEAD_DIM)] for n in range(2)], axis=0)
        scores = lax.dot_general(
            both, keys, (((1,), (1,)), ((), ())), preferred_element_type=jnp.float32)
        qtimes = jnp.concatenate([qtime, qtime], axis=0)
        scores = jnp.where(ktime[0:1, :] <= qtimes, scores * (score_scale * LOG2E), NEG)
        peak = jnp.max(scores, axis=1, keepdims=True)
        terms = jnp.exp2(scores - peak)
        total = jnp.sum(terms, axis=1, keepdims=True)
        mixed = jnp.dot(terms.astype(jnp.bfloat16), values, preferred_element_type=jnp.float32)
        mixed = (mixed / total).astype(jnp.bfloat16)
        lse = jnp.where(peak > 0.5 * NEG, peak + jnp.log2(total), NEG)
        for n in range(2):
            rows = slice(n * ROWS, (n + 1) * ROWS)
            obuf[d, :, pl.ds(n * HEAD_DIM, HEAD_DIM)] = mixed[rows]
            lbuf[d, pl.ds(n * 8, 8)] = to_row(lse[rows])

        @pl.when(d > 0)
        def _():
            o_copy(d).start()
            l_copy(d).start()

        return carry

    lax.fori_loop(0, Y, attend, 0)
    oin[0] = obuf[0]
    lin[0] = lbuf[0]
    for d in range(1, Y):
        o_copy(d).wait_recv()
        l_copy(d).wait_recv()
    top = jnp.maximum(jnp.maximum(lin[0], lin[1]), jnp.maximum(lin[2], lin[3]))
    weights = [jnp.exp2(lin[d] - top) for d in range(Y)]
    norm = 1.0 / ((weights[0] + weights[1]) + (weights[2] + weights[3]))
    for n in range(2):
        span = pl.ds(n * HEAD_DIM, HEAD_DIM)
        result = None
        for d in range(Y):
            w = to_cols((weights[d] * norm)[n * 8:n * 8 + 1, :])
            part = w * oin[d, :, span].astype(jnp.float32)
            result = part if result is None else result + part
        out[:, span] = result.astype(jnp.bfloat16)

    for copy in w_live.values():
        copy.wait_send()
    for copy in sends:
        copy.wait_send()
    for d in range(1, Y):
        qa_copy(d).wait_send()
        o_copy(d).wait_send()
        l_copy(d).wait_send()


def body(activations, w_query, w_keyval, q_gain, k_gain, stream_ids, local_times, block_map):
    bf, f32 = jnp.bfloat16, jnp.float32
    vmem = pl.BlockSpec(memory_space=pltpu.VMEM)
    anywhere = pl.BlockSpec(memory_space=pl.ANY)
    dma = pltpu.SemaphoreType.DMA
    scratch = [
        pltpu.VMEM((ROWS, 4096), bf),
        pltpu.VMEM((STREAMS, 2 * HEAD_DIM), f32),
        pltpu.VMEM((STREAMS, KV_HEADS * HEAD_DIM), f32),
        pltpu.VMEM((1, ROWS), jnp.int32),
        pltpu.VMEM((1, ROWS), jnp.int32),
        pltpu.VMEM((1, ROWS), jnp.int32),
        pltpu.VMEM((ROWS, META), bf),
        pltpu.VMEM((Y, ROWS, DEPTH + META), bf),
        pltpu.VMEM((Y, ROWS, DEPTH + META), bf),
        pltpu.VMEM((STREAMS, DEPTH, 2 * HEAD_DIM), bf),
        pltpu.VMEM((DEPTH, STREAMS * HEAD_DIM), bf),
        pltpu.VMEM((STREAMS, Y * ROWS, 256), bf),
        pltpu.VMEM((Y, ROWS, HEAD_DIM), f32),
        pltpu.VMEM((Y, ROWS, 2 * HEAD_DIM), f32),
        pltpu.VMEM((Y - 1, ROWS, HEAD_DIM), f32),
        pltpu.VMEM((Y - 1, ROWS, 2 * HEAD_DIM), f32),
        pltpu.VMEM((X, 8, ROWS), f32),
        pltpu.VMEM((2 * X, 8, ROWS), f32),
        pltpu.VMEM((2, Z, ROWS, HEAD_DIM), bf),
        pltpu.VMEM((Z, 16, ROWS), bf),
        pltpu.VMEM((Y, ROWS, 2 * HEAD_DIM), bf),
        pltpu.VMEM((8, KEYS), f32),
        pltpu.VMEM((Y, ROWS, 2 * HEAD_DIM), bf),
        pltpu.VMEM((Y, ROWS, 2 * HEAD_DIM), bf),
        pltpu.VMEM((Y, 16, ROWS), f32),
        pltpu.VMEM((Y, 16, ROWS), f32),
        dma((10,)),
        dma((2, Z // 2, STREAMS + 2)), dma((2, Z // 2, STREAMS + 2)),
    ]
    for n in (3, 3, 3, 3, 3, 7, Z + 1, Z, 4, 4, 4):
        scratch += [dma((n,)), dma((n,))]
    return pl.pallas_call(
        kernel,
        out_shape=pltpu.VMEM((ROWS, 2 * HEAD_DIM), bf),
        in_specs=[anywhere] * 8,
        out_specs=vmem,
        scratch_shapes=scratch,
        compiler_params=pltpu.CompilerParams(
            collective_id=0, has_side_effects=True, vmem_limit_bytes=56 << 20),
        name="duplex_attention",
    )(
        activations, w_query, w_keyval, q_gain, k_gain,
        stream_ids.reshape(1, ROWS), local_times.reshape(1, ROWS), block_map.reshape(1, ROWS),
    )


def solution(mesh):
    placed = (
        P("seq", None),
        P(None, "seq", "head"),
        P(None, "seq", None),
        P(None, "head"),
        P(),
        P("seq"),
        P("seq"),
        P(),
    )
    return jax.shard_map(
        body, mesh=mesh, in_specs=placed, out_specs=P("seq", "head"), check_vma=False
    )
```

```python
import math

import jax
import jax.numpy as jnp
from jax import lax
from jax.experimental import pallas as pl
from jax.experimental.pallas import tpu as pltpu
from jax.sharding import PartitionSpec as P

HEADS = 16
KV_HEADS = 4
HEAD_DIM = 128
STREAMS = 3
FRAMES = 32
EPS = 1e-06
MESH = pl.DeviceIdType.MESH

Z, Y, X = 16, 4, 4
ROWS = 128
SHARD = 64
HALF = ROWS // 2
DEPTH = Z * SHARD
META = 128
KEYS = Z * ROWS
NEG = -1e30
LOG2E = 1.0 / math.log(2.0)

ORDER = [0]
for _k in range(1, Z // 2):
    ORDER += [_k, -_k]
ORDER.append(Z // 2)
POS = {o: i for i, o in enumerate(ORDER)}
POS[-Z // 2] = POS[Z // 2]


def to_row(col):
    return jnp.transpose(jnp.broadcast_to(col, (ROWS, 128)))[0:8, :]


def to_cols(row):
    return jnp.transpose(jnp.broadcast_to(row, (128, ROWS)))


def kernel(
    x_hbm, wq_hbm, wkv_hbm, qg_hbm, kg_hbm, ids_hbm, times_hbm, map_hbm, out,
    xv, qgain, kgain, ids, times, places, meta, xpk, xall, wall, wkv, hot, acc_kv, acc_q, in_kv, in_q, statk, statq,
    kv2, when, qall, ktime, obuf, oin, lbuf, lin,
    load_sem, w_ss, w_rs, x_ss, x_rs, xp_ss, xp_rs, kv_ss, kv_rs, q_ss, q_rs,
    sk_ss, sk_rs, sq_ss, sq_rs, g_ss, g_rs, p_ss, p_rs, qa_ss, qa_rs,
    o_ss, o_rs, l_ss, l_rs,
):
    h = lax.axis_index("head")
    s = lax.axis_index("seq")
    x, c = h // 2, h % 2
    z, y = s // Y, s % Y

    def zdev(d):
        return (h, lax.rem(z + d + Z, Z) * Y + y)

    def ydev(d):
        return (h, z * Y + lax.rem(y + d + Y, Y))

    def hdev(d):
        return (lax.rem(h + d, 2 * X), s)

    def xdev(d):
        return (lax.rem(h + 2 * d, 2 * X), s)

    partner = (2 * x + 1 - c, s)

    def remote(src, dst, ss, rs, dev):
        return pltpu.make_async_remote_copy(
            src_ref=src, dst_ref=dst, send_sem=ss, recv_sem=rs,
            device_id=dev, device_id_type=MESH,
        )

    kv_off = pl.multiple_of((2 * x + c) * HEAD_DIM, HEAD_DIM)
    w_loads = [
        (wkv_hbm.at[j, :, pl.ds(kv_off, HEAD_DIM)],
         wkv.at[pl.ds(0, SHARD), pl.ds(j * HEAD_DIM, HEAD_DIM)])
        for j in range(STREAMS)
    ]
    w_loads.append((wq_hbm, wall.at[:, pl.ds(0, SHARD)]))
    row_loads = [
        (x_hbm, xv), (ids_hbm, ids), (times_hbm, times), (map_hbm, places),
        (qg_hbm, qgain), (kg_hbm, kgain),
    ]
    loads = [
        pltpu.make_async_copy(src, dst, load_sem.at[i])
        for i, (src, dst) in enumerate(w_loads + row_loads)
    ]
    for load in loads:
        load.start()
    barrier = pltpu.get_barrier_semaphore()
    peers = [zdev(d) for d in (1, -1)]
    peers += [ydev(d) for d in (1, 2, 3)]
    peers += [hdev(d) for d in range(1, 2 * X)]
    for dev in peers:
        pl.semaphore_signal(barrier, inc=1, device_id=dev, device_id_type=MESH)
    for load in loads[:len(w_loads)]:
        load.wait()
    pl.semaphore_wait(barrier, len(peers))

    sends = []

    def sent(copy):
        copy.start()
        sends.append(copy)
        return copy

    class Spread:
        def __init__(self, piece, ss, rs):
            self.piece, self.ss, self.rs, self.live = piece, ss, rs, {}

        def send(self, have, step, part=0, index=None):
            o = have - step
            o = o - Z if o > Z // 2 else o
            i = POS[o] if index is None else index
            self.live[i] = sent(remote(
                self.piece(POS[have], part), self.piece(POS[o], part),
                self.ss.at[i], self.rs.at[i], zdev(step)))

        def wait(self, o):
            self.live[POS[o]].wait_recv()

        def first(self):
            for step in (6, -6, 3, -3, 1, -1):
                self.send(0, step)

        def second(self):
            for o in (3, -3):
                self.wait(o)
                self.send(o, 1)
                self.send(o, -1)

        def third(self):
            for o in (6, -6):
                self.wait(o)
                self.send(o, 1)
                self.send(o, -1)
            self.send(6, -2, 1, Z - 1)
            self.send(-6, 2, 2, Z)

        def wait_last(self):
            self.live[Z - 1].wait_recv()
            self.live[Z].wait_recv()

    def kv_piece(i, part):
        start, size = ((0, ROWS), (0, HALF), (HALF, HALF))[part]
        return kv2.at[c, i, pl.ds(start, size)]

    kv_spread = Spread(kv_piece, g_ss, g_rs)

    def w_piece(i, j):
        span = pl.ds(i * SHARD, SHARD)
        if j == STREAMS + 1:
            return when.at[i]
        return wkv.at[span] if j == 0 else wall.at[j - 1, span]

    def w_copy(k, j, up):
        sign = -1 if up else 1
        src, dst = w_piece(POS[sign * (k - 1)], j), w_piece(POS[sign * k], j)
        i = 0 if up else 1
        return remote(src, dst, w_ss.at[i, k - 1, j], w_rs.at[i, k - 1, j], zdev(1 if up else -1))

    last = Z // 2
    ways = {}
    for k in range(1, last):
        ways[k] = [(j, up) for j in range(STREAMS + 2) for up in (True, False)]
    ways[last] = [(0, True), (1, False), (2, True), (3, False), (4, True)]
    w_live = {}

    def w_step(k, chunks=range(STREAMS + 2)):
        for j, up in ways[k]:
            if j not in chunks:
                continue
            if k > 1:
                w_live[(k - 1, j, up)].wait_recv()
            w_live[(k, j, up)] = w_copy(k, j, up)
            w_live[(k, j, up)].start()

    def w_done(j):
        for k in (last - 1, last):
            for i, up in ways[k]:
                if i == j and (k == last or (j, up) not in ways[last]):
                    w_live[(k, j, up)].wait_recv()

    w_step(1, range(STREAMS + 1))
    for load in loads[len(w_loads):]:
        load.wait()

    lane = lax.broadcasted_iota(jnp.int32, (ROWS, META), 1)
    row_lane = lax.broadcasted_iota(jnp.int32, (1, ROWS), 1)
    block_places = places[...].astype(jnp.float32)
    first, second = [
        jnp.sum(jnp.where(row_lane == 2 * s + i, block_places, 0.0), axis=1, keepdims=True)
        for i in range(2)
    ]
    place_row = jnp.where(row_lane < HALF, first, second)
    time_row = times[...].astype(jnp.float32)
    id_col = to_cols(ids[...].astype(jnp.float32))
    meta[...] = jnp.where(
        lane < 32, id_col, jnp.where(lane < 64, to_cols(time_row), to_cols(place_row))
    ).astype(jnp.bfloat16)

    line = lax.broadcasted_iota(jnp.int32, (16, ROWS), 0)
    when[0] = jnp.where(line == 0, time_row, place_row).astype(jnp.bfloat16)
    w_step(1, (STREAMS + 1,))

    for t in range(Y):
        half = t % 2
        for pair in range(Z // 2):
            parts = []
            for o in (ORDER[2 * pair], ORDER[2 * pair + 1]):
                tile = 2 * lax.rem(z + o + Z, Z) + t // 2
                block = xv[:, pl.ds(pl.multiple_of(tile * 128, 128), 128)]
                parts.append(block[:, half * SHARD:(half + 1) * SHARD])
            xpk[t, :, pl.ds(pair * 128, 128)] = jnp.concatenate(parts, axis=1)
        xpk[t, :, pl.ds(DEPTH, META)] = meta[...]
    my_half = pl.ds(pl.multiple_of(c * HALF, HALF), HALF)
    x_live = {}
    for d in (2, 1, 3):
        x_live[d] = sent(remote(
            xpk.at[lax.rem(y + d, Y), my_half], xall.at[d, my_half],
            x_ss.at[d - 1], x_rs.at[d - 1], ydev(d)))
    xall[0] = xpk[y]
    w_step(2)
    w_step(3)
    xp_live = []
    for d in (1, 3, 2):
        x_live[d].wait_recv()
        xp_live.append(sent(remote(
            xall.at[d, my_half], xall.at[d, my_half],
            xp_ss.at[d - 1], xp_rs.at[d - 1], partner)))
    w_step(4)
    for copy in xp_live:
        copy.wait_recv()
    for d in range(Y):
        sid = xall[d, :, pl.ds(DEPTH, META)][:, 0:1].astype(jnp.float32)
        for j in range(STREAMS):
            on = jnp.where(sid == jnp.float32(j), jnp.float32(1.0), jnp.float32(0.0))
            hot[j, pl.ds(d * ROWS, ROWS)] = jnp.broadcast_to(on, (ROWS, 256)).astype(jnp.bfloat16)
    w_step(5)

    def project(g):
        span = pl.ds(g * 256, 256)
        for d in range(Y):
            xs = xall[d, :, span]
            total = None
            for j in range(STREAMS):
                part = jnp.dot(
                    xs * hot[j, pl.ds(d * ROWS, ROWS)], wall[j, span, :],
                    preferred_element_type=jnp.float32)
                total = part if total is None else total + part
            if g == 0:
                acc_q[d] = total
            else:
                acc_q[d] += total

    def project_kv(d, span):
        sid = xall[d, :, pl.ds(DEPTH, META)][:, 0:1].astype(jnp.float32)
        every = jnp.dot(xall[d, :, span], wkv[span, :], preferred_element_type=jnp.float32)
        part = every[:, :HEAD_DIM]
        for j in range(1, STREAMS):
            part = jnp.where(
                sid == jnp.float32(j), every[:, j * HEAD_DIM:(j + 1) * HEAD_DIM], part)
        return part

    early, late = pl.ds(0, DEPTH - 256), pl.ds(DEPTH - 256, 256)
    w_step(6)
    project(0)
    w_step(7)
    w_step(8)
    for d in range(Y):
        acc_kv[d] = project_kv(d, early)
    project(1)
    project(2)
    k_scale = jnp.zeros((ROWS, HEAD_DIM), jnp.float32)
    q_scale = jnp.zeros((ROWS, 2 * HEAD_DIM), jnp.float32)
    sid = meta[:, 0:1].astype(jnp.float32)
    group = pl.ds(pl.multiple_of(x * HEAD_DIM, HEAD_DIM), HEAD_DIM)
    for j in range(STREAMS):
        k_scale = jnp.where(sid == jnp.float32(j), kgain[j:j + 1, group], k_scale)
        q_scale = jnp.where(sid == jnp.float32(j), qgain[j:j + 1, :], q_scale)

    w_done(0)
    kv_live, q_live = [], []
    for d in (2, 1, 3, 0):
        acc_kv[d] += project_kv(d, late)
        if d:
            kv_live.append(sent(remote(
                acc_kv.at[d], in_kv.at[d - 1], kv_ss.at[d - 1], kv_rs.at[d - 1], ydev(-d))))
    for j in range(STREAMS + 1):
        w_done(j + 1)
    project(3)
    for d in (2, 1, 3):
        q_live.append(sent(remote(
            acc_q.at[d], in_q.at[d - 1], q_ss.at[d - 1], q_rs.at[d - 1], ydev(-d))))
    for copy in kv_live:
        copy.wait_recv()
    kv = (acc_kv[0] + in_kv[0]) + (in_kv[1] + in_kv[2])
    statk[0] = to_row(jnp.sum(kv * kv, axis=1, keepdims=True))
    sk_live = []
    for d in (2, 1, 3):
        sk_live.append(sent(remote(
            statk.at[0], statk.at[d], sk_ss.at[d - 1], sk_rs.at[d - 1], xdev(d))))
    for copy in sk_live:
        copy.wait_recv()
    k_sq = (statk[0] + statk[1]) + (statk[2] + statk[3])
    k_rs = to_cols(lax.rsqrt(k_sq / (KV_HEADS * HEAD_DIM) + EPS)[0:1, :])
    is_key = c == 0
    normed = jnp.where(is_key, kv * k_rs * k_scale, kv)
    kv2[c, 0] = normed.astype(jnp.bfloat16)

    p_live = {}

    def p_send(have):
        i = POS[have]
        p_live[i] = sent(remote(kv2.at[c, i], kv2.at[c, i], p_ss.at[i], p_rs.at[i], partner))

    kv_spread.first()
    p_send(0)
    for copy in q_live:
        copy.wait_recv()
    q = (acc_q[0] + in_q[0]) + (in_q[1] + in_q[2])
    statq[0] = to_row(jnp.sum(q * q, axis=1, keepdims=True))
    sq_live = []
    for d in range(1, 2 * X):
        sq_live.append(sent(remote(
            statq.at[0], statq.at[d], sq_ss.at[d - 1], sq_rs.at[d - 1], hdev(d))))
    for i in range(Z):
        km = when[i].astype(jnp.float32)
        ktime[0:1, pl.ds(i * ROWS, ROWS)] = km[1:2, :] * FRAMES + km[0:1, :]
    for copy in sq_live:
        copy.wait_recv()
    q_sq = statq[0]
    for d in range(1, 2 * X):
        q_sq = q_sq + statq[d]
    q_rs = to_cols(lax.rsqrt(q_sq / (HEADS * HEAD_DIM) + EPS)[0:1, :])
    q_rs = jnp.concatenate([q_rs, q_rs], axis=1)
    qall[0] = (q * q_rs * q_scale).astype(jnp.bfloat16)

    def qa_copy(d):
        return remote(qall.at[0], qall.at[d], qa_ss.at[d], qa_rs.at[d], ydev(d))

    for d in (2, 1, 3):
        qa_copy(d).start()
    kv_spread.second()
    p_send(3)
    p_send(-3)
    for o in (1, -1):
        kv_spread.wait(o)
        p_send(o)
    kv_spread.third()
    p_send(6)
    p_send(-6)
    for o in (2, 4, -2, -4, 5, 7, -5, -7):
        kv_spread.wait(o)
        p_send(o)
    kv_spread.wait_last()
    p_send(Z // 2)
    for copy in p_live.values():
        copy.wait_recv()

    score_scale = 1.0 / math.sqrt(HEAD_DIM)

    def o_copy(d):
        return remote(obuf.at[d], oin.at[d], o_ss.at[d], o_rs.at[d], ydev(-d))

    def l_copy(d):
        return remote(lbuf.at[d], lin.at[d], l_ss.at[d], l_rs.at[d], ydev(-d))

    def attend(i, carry):
        d = Y - 1 - i

        @pl.when(d > 0)
        def _():
            qa_copy(d).wait_recv()

        qm = xall[d, :, pl.ds(DEPTH, META)].astype(jnp.float32)
        qtime = qm[:, 64:65] * FRAMES + qm[:, 32:33]
        keys = kv2[0].reshape(KEYS, HEAD_DIM)
        values = kv2[1].reshape(KEYS, HEAD_DIM)
        both = jnp.concatenate(
            [qall[d, :, pl.ds(n * HEAD_DIM, HEAD_DIM)] for n in range(2)], axis=0)
        scores = lax.dot_general(
            both, keys, (((1,), (1,)), ((), ())), preferred_element_type=jnp.float32)
        qtimes = jnp.concatenate([qtime, qtime], axis=0)
        scores = jnp.where(ktime[0:1, :] <= qtimes, scores * (score_scale * LOG2E), NEG)
        peak = jnp.max(scores, axis=1, keepdims=True)
        terms = jnp.exp2(scores - peak)
        total = jnp.sum(terms, axis=1, keepdims=True)
        mixed = jnp.dot(terms.astype(jnp.bfloat16), values, preferred_element_type=jnp.float32)
        mixed = (mixed / total).astype(jnp.bfloat16)
        lse = jnp.where(peak > 0.5 * NEG, peak + jnp.log2(total), NEG)
        for n in range(2):
            rows = slice(n * ROWS, (n + 1) * ROWS)
            obuf[d, :, pl.ds(n * HEAD_DIM, HEAD_DIM)] = mixed[rows]
            lbuf[d, pl.ds(n * 8, 8)] = to_row(lse[rows])

        @pl.when(d > 0)
        def _():
            o_copy(d).start()
            l_copy(d).start()

        return carry

    lax.fori_loop(0, Y, attend, 0)
    oin[0] = obuf[0]
    lin[0] = lbuf[0]
    for d in range(1, Y):
        o_copy(d).wait_recv()
        l_copy(d).wait_recv()
    top = jnp.maximum(jnp.maximum(lin[0], lin[1]), jnp.maximum(lin[2], lin[3]))
    weights = [jnp.exp2(lin[d] - top) for d in range(Y)]
    norm = 1.0 / ((weights[0] + weights[1]) + (weights[2] + weights[3]))
    for n in range(2):
        span = pl.ds(n * HEAD_DIM, HEAD_DIM)
        result = None
        for d in range(Y):
            w = to_cols((weights[d] * norm)[n * 8:n * 8 + 1, :])
            part = w * oin[d, :, span].astype(jnp.float32)
            result = part if result is None else result + part
        out[:, span] = result.astype(jnp.bfloat16)

    for copy in w_live.values():
        copy.wait_send()
    for copy in sends:
        copy.wait_send()
    for d in range(1, Y):
        qa_copy(d).wait_send()
        o_copy(d).wait_send()
        l_copy(d).wait_send()


def body(activations, w_query, w_keyval, q_gain, k_gain, stream_ids, local_times, block_map):
    bf, f32 = jnp.bfloat16, jnp.float32
    vmem = pl.BlockSpec(memory_space=pltpu.VMEM)
    anywhere = pl.BlockSpec(memory_space=pl.ANY)
    dma = pltpu.SemaphoreType.DMA
    scratch = [
        pltpu.VMEM((ROWS, 4096), bf),
        pltpu.VMEM((STREAMS, 2 * HEAD_DIM), f32),
        pltpu.VMEM((STREAMS, KV_HEADS * HEAD_DIM), f32),
        pltpu.VMEM((1, ROWS), jnp.int32),
        pltpu.VMEM((1, ROWS), jnp.int32),
        pltpu.VMEM((1, ROWS), jnp.int32),
        pltpu.VMEM((ROWS, META), bf),
        pltpu.VMEM((Y, ROWS, DEPTH + META), bf),
        pltpu.VMEM((Y, ROWS, DEPTH + META), bf),
        pltpu.VMEM((STREAMS, DEPTH, 2 * HEAD_DIM), bf),
        pltpu.VMEM((DEPTH, STREAMS * HEAD_DIM), bf),
        pltpu.VMEM((STREAMS, Y * ROWS, 256), bf),
        pltpu.VMEM((Y, ROWS, HEAD_DIM), f32),
        pltpu.VMEM((Y, ROWS, 2 * HEAD_DIM), f32),
        pltpu.VMEM((Y - 1, ROWS, HEAD_DIM), f32),
        pltpu.VMEM((Y - 1, ROWS, 2 * HEAD_DIM), f32),
        pltpu.VMEM((X, 8, ROWS), f32),
        pltpu.VMEM((2 * X, 8, ROWS), f32),
        pltpu.VMEM((2, Z, ROWS, HEAD_DIM), bf),
        pltpu.VMEM((Z, 16, ROWS), bf),
        pltpu.VMEM((Y, ROWS, 2 * HEAD_DIM), bf),
        pltpu.VMEM((8, KEYS), f32),
        pltpu.VMEM((Y, ROWS, 2 * HEAD_DIM), bf),
        pltpu.VMEM((Y, ROWS, 2 * HEAD_DIM), bf),
        pltpu.VMEM((Y, 16, ROWS), f32),
        pltpu.VMEM((Y, 16, ROWS), f32),
        dma((10,)),
        dma((2, Z // 2, STREAMS + 2)), dma((2, Z // 2, STREAMS + 2)),
    ]
    for n in (3, 3, 3, 3, 3, 7, Z + 1, Z, 4, 4, 4):
        scratch += [dma((n,)), dma((n,))]
    return pl.pallas_call(
        kernel,
        out_shape=pltpu.VMEM((ROWS, 2 * HEAD_DIM), bf),
        in_specs=[anywhere] * 8,
        out_specs=vmem,
        scratch_shapes=scratch,
        compiler_params=pltpu.CompilerParams(
            collective_id=0, has_side_effects=True, vmem_limit_bytes=56 << 20),
        name="duplex_attention",
    )(
        activations, w_query, w_keyval, q_gain, k_gain,
        stream_ids.reshape(1, ROWS), local_times.reshape(1, ROWS), block_map.reshape(1, ROWS),
    )


def solution(mesh):
    placed = (
        P("seq", None),
        P(None, "seq", "head"),
        P(None, "seq", None),
        P(None, "head"),
        P(),
        P("seq"),
        P("seq"),
        P(),
    )
    return jax.shard_map(
        body, mesh=mesh, in_specs=placed, out_specs=P("seq", "head"), check_vma=False
    )
```
